32 devices in a mesh: rep: 4 (over z), fsdp: 8 (over y, x, core).
Axes of the slice: x: 2, y: 2, z: 4, core: 2. Of those that a mesh axis runs over, the one named last changes fastest.
Arguments:
- hidden: bfloat16 [4096, 8192], P(('rep', 'fsdp')), may hold values from -6 to 6
- gain: float32 [8192], replicated, may hold values from 0.1 to 1.9
- key_weight: bfloat16 [4, 8192, 512], P('rep', 'fsdp'), may hold values from -6 to 6
- moment: float32 [4, 8192, 512], P('rep', 'fsdp'), may hold values from -4 to 4
- second: float32 [4, 8192, 512], P('rep', 'fsdp'), may hold values from 0.05 to 1
- dkeys: bfloat16 [4096, 512], P(('rep', 'fsdp')), may hold values from -6 to 6
- step: int32 [], replicated, may hold values from 0 to 29
Outputs:
- keys: bfloat16 [4096, 512], P(('rep', 'fsdp'))
- new_weight: bfloat16 [4, 8192, 512], P('rep', 'fsdp')
- new_moment: float32 [4, 8192, 512], P('rep', 'fsdp')
- new_second: float32 [4, 8192, 512], P('rep', 'fsdp')
The draws below stay inside these ranges and needn't reach their ends.
All inputs are finite; a program needn't handle non-finite values.
Results may differ from the reference program's by a relative error of at most 0.0051.
Values may be sent and summed in bfloat16 or wider, within the bound.
A program may use at most 64 MiB of HBM per device.

```python
import math
import jax
import jax.numpy as jnp
from jax import lax

D = 8192
HEAD = 128
TOK_DEV = 128
KVW = 512
TOKENS = 4096
N_REP = 4
N_FSDP = 8


def strengthened(drawn, key, source, target, shards_of, factor):
    def block_of(dim):
        return (jnp.arange(drawn.shape[dim]) // (drawn.shape[dim] // shards_of)).reshape((-1,) + (1,) * (drawn.ndim - 1 - dim))

    near = jax.random.permutation(key, shards_of)[block_of(target)]
    second = (block_of(target) + shards_of // 2) % shards_of
    return jnp.where((block_of(source) == near) | (block_of(source) == second), factor * drawn, drawn)


def levels(rng, dims, pieces, low, largest):
    def one(axis_at, blocks):
        heights = jax.random.uniform(jax.random.fold_in(jax.random.fold_in(rng, 6), axis_at), (blocks,), jnp.float32, low / len(pieces), largest / len(pieces))
        return jnp.repeat(jnp.exp(heights), dims[axis_at] // blocks).reshape((-1,) + (1,) * (len(dims) - axis_at - 1))

    loudness = one(*pieces[0])
    for cut in pieces[1:]:
        loudness = loudness * one(*cut)
    return loudness


def centred(stream_key, shape, width, reach, cuts=(), kind=jnp.bfloat16):
    entries = width * jax.random.normal(stream_key, shape, jnp.float32)
    if cuts:
        entries = entries * levels(stream_key, shape, cuts, -0.22, 0.18)
    return jnp.clip(entries, -reach, reach).astype(kind)


def noise_with(stream_key, dims, spread, bound, pieces, heavy, held_as=jnp.bfloat16):
    values = spread * jax.random.normal(stream_key, dims, jnp.float32)
    if pieces:
        values = values * levels(stream_key, dims, pieces, -0.22, 0.18)
    return jnp.clip(strengthened(values, jax.random.fold_in(stream_key, 3), *heavy), -bound, bound).astype(held_as)


def setup_inputs(seed: int = 0) -> dict:
    keys = jax.random.split(jax.random.key(seed), 8)
    hidden = noise_with(keys[0], (TOKENS, D), 1.0, 6.0, ((0, 32),), (0, 1, 32, 2.75))
    gain = jnp.clip(1.0 + 0.18 * jax.random.normal(keys[1], (D,), jnp.float32), 0.1, 1.9)
    key_weight = centred(keys[2], (N_REP, D, KVW), 1.0, 6.0, ((0, 4), (1, 8)))
    moment = centred(keys[3], (N_REP, D, KVW), 0.3, 4.0, ((0, 4), (1, 8)), jnp.float32)
    second = jnp.clip(jnp.exp(math.log(1.0) - 2.9957323 * jax.random.uniform(keys[4], (N_REP, D, KVW), jnp.float32) ** levels(keys[4], (N_REP, D, KVW), ((0, 4), (1, 8)), -0.2, 0.2)), 0.05, 1.0)
    dkeys = centred(keys[5], (TOKENS, KVW), 1.0, 6.0, ((0, 32),))
    step = jax.random.randint(keys[6], (), 0, 30).astype(jnp.int32)
    return {"hidden": hidden, "gain": gain, "key_weight": key_weight, "moment": moment, "second": second, "dkeys": dkeys, "step": step}


def rotate(values, positions, sign):
    count = values.shape[0]
    heads = values.reshape(count, -1, HEAD)
    half = HEAD // 2
    freq = jnp.exp(jnp.arange(half).astype(jnp.float32) * (-2.0 * math.log(500000.0) / HEAD))
    angle = positions.astype(jnp.float32)[:, None] * freq[None, :]
    cosine = jnp.cos(angle)[:, None, :]
    sine = jnp.sin(angle)[:, None, :]
    first = heads[..., :half]
    latter = heads[..., half:]
    turned = jnp.concatenate([first * cosine - sign * latter * sine, latter * cosine + sign * first * sine], axis=-1)
    return turned.reshape(count, -1)

def reference(hidden, gain, key_weight, moment, second, dkeys, step):
    group_rows = TOK_DEV * N_FSDP
    scale = D ** (-0.5)
    positions = jnp.arange(group_rows).astype(jnp.int32)

    def one_group(items):
        rows, weight, cotangent = items
        values = rows.astype(jnp.float32)
        inverse = lax.rsqrt(lax.optimization_barrier(jnp.mean(values * values, axis=-1, keepdims=True)) + 1e-05)
        normed = (values * inverse * gain).astype(jnp.bfloat16)
        pre = jnp.dot(normed, weight, preferred_element_type=jnp.float32) * scale
        turned = rotate(pre, positions, 1.0).astype(jnp.bfloat16)
        dpre = rotate(cotangent.astype(jnp.float32), positions, -1.0).astype(jnp.bfloat16)
        grad = lax.dot_general(normed, dpre, (((0,), (0,)), ((), ())), preferred_element_type=jnp.float32) * scale
        return (turned, grad)
    turned, grads = lax.map(one_group, (hidden.reshape(N_REP, group_rows, D), key_weight, dkeys.reshape(N_REP, group_rows, KVW)))
    count = (step + 1).astype(jnp.float32)
    new_moment = 0.9 * moment + 0.1 * grads
    new_second = 0.95 * second + 0.05 * grads * grads
    mhat = new_moment / (1.0 - jnp.power(jnp.float32(0.9), count))
    vhat = new_second / (1.0 - jnp.power(jnp.float32(0.95), count))
    weight32 = key_weight.astype(jnp.float32)
    local = (weight32 - 0.05 * (mhat / (jnp.sqrt(vhat) + 1e-08) + 0.1 * weight32)).astype(jnp.bfloat16)
    phase = step % 3
    distance = jnp.where(phase == 0, 1, jnp.where(phase == 1, 2, 4)).astype(jnp.int32) % N_REP
    partner_index = (jnp.arange(N_REP).astype(jnp.int32) - distance) % N_REP
    other = jnp.take(local, partner_index, axis=0)
    new_weight = ((local.astype(jnp.float32) + other.astype(jnp.float32)) * 0.5).astype(jnp.bfloat16)
    return (turned.reshape(TOKENS, KVW), new_weight, new_moment, new_second)
```

```python
import math

import jax
import jax.numpy as jnp
from jax import lax
from jax.sharding import PartitionSpec as P

HEAD = 128


def as_sent(x):

    def short(part):
        return part.astype(jnp.bfloat16) if part.dtype == jnp.float32 else part

    return jax.tree.map(short, x)


def from_behind(block, axis, distance):
    devices = range(lax.axis_size(axis))
    route = [((i - distance) % len(devices), i) for i in devices]
    return lax.ppermute(block, axis, route)


def rotate(values, positions, sign):
    count = values.shape[0]
    heads = values.reshape(count, -1, HEAD)
    half = HEAD // 2
    freq = jnp.exp(jnp.arange(half).astype(jnp.float32) * (-2.0 * math.log(500000.0) / HEAD))
    angle = positions.astype(jnp.float32)[:, None] * freq[None, :]
    cosine = jnp.cos(angle)[:, None, :]
    sine = jnp.sin(angle)[:, None, :]
    first = heads[..., :half]
    latter = heads[..., half:]
    turned = jnp.concatenate(
        [first * cosine - sign * latter * sine, latter * cosine + sign * first * sine], axis=-1
    )
    return turned.reshape(count, -1)


def from_partner(values, offset):
    if offset == 0:
        return values
    return jax.tree.map(
        lambda part, own: part.astype(own.dtype),
        from_behind(as_sent(values), "rep", offset),
        values,
    )


def per_device(hidden, gain, key_weight, moment, second, dkeys, step):
    tok_rows = hidden.shape[0]
    width = hidden.shape[1]
    scale = width ** (-0.5)
    weight = key_weight[0]
    values = hidden.astype(jnp.float32)
    inverse = lax.rsqrt(jnp.mean(values * values, axis=-1, keepdims=True) + 1e-05)
    normed = (values * inverse * gain).astype(jnp.bfloat16)
    positions = lax.axis_index("fsdp") * tok_rows + jnp.arange(tok_rows)
    dpre = rotate(dkeys.astype(jnp.float32), positions, -1.0).astype(jnp.bfloat16)
    slices = lax.all_to_all(normed, "fsdp", split_axis=1, concat_axis=0, tiled=True)
    partial = jnp.dot(slices, weight, preferred_element_type=jnp.float32).astype(jnp.bfloat16)
    shares = lax.all_to_all(
        partial.reshape(-1, tok_rows, partial.shape[1]),
        "fsdp",
        split_axis=0,
        concat_axis=0,
        tiled=True,
    )
    pre = jnp.sum(shares.astype(jnp.float32), axis=0) * scale
    turned = rotate(pre, positions, 1.0).astype(jnp.bfloat16)
    gathered = lax.all_gather(dpre, "fsdp", axis=0, tiled=True)
    total = lax.dot_general(
        slices, gathered, (((0,), (0,)), ((), ())), preferred_element_type=jnp.float32
    )
    grad = total * scale
    count = (step + 1).astype(jnp.float32)
    new_moment = 0.9 * moment[0] + 0.1 * grad
    new_second = 0.95 * second[0] + 0.05 * grad * grad
    mhat = new_moment / (1.0 - jnp.power(jnp.float32(0.9), count))
    vhat = new_second / (1.0 - jnp.power(jnp.float32(0.95), count))
    weight32 = weight.astype(jnp.float32)
    local = (weight32 - 0.05 * (mhat / (jnp.sqrt(vhat) + 1e-08) + 0.1 * weight32)).astype(
        jnp.bfloat16
    )
    groups = lax.axis_size("rep")
    other = lax.switch(
        step % 3,
        [
            lambda values: from_partner(values, 1 % groups),
            lambda values: from_partner(values, 2 % groups),
            lambda values: from_partner(values, 4 % groups),
        ],
        local,
    )
    new_weight = ((local.astype(jnp.float32) + other.astype(jnp.float32)) * 0.5).astype(
        jnp.bfloat16
    )
    return (turned, new_weight[None], new_moment[None], new_second[None])


def solution(mesh):
    return jax.shard_map(
        per_device,
        mesh=mesh,
        in_specs=(
            P(("rep", "fsdp"), None),
            P(),
            P("rep", "fsdp", None),
            P("rep", "fsdp", None),
            P("rep", "fsdp", None),
            P(("rep", "fsdp"), None),
            P(),
        ),
        out_specs=(
            P(("rep", "fsdp"), None),
            P("rep", "fsdp", None),
            P("rep", "fsdp", None),
            P("rep", "fsdp", None),
        ),
        check_vma=False,
    )
```

```python
import functools
import math

import jax
import jax.numpy as jnp
from jax import lax
from jax.experimental import pallas as pl
from jax.experimental.pallas import tpu as pltpu
from jax.sharding import PartitionSpec as P

HEAD = 128
LANES = 128
CHUNKS = 4
MESH = pl.DeviceIdType.MESH
bf16 = jnp.bfloat16
f32 = jnp.float32


def loop(low, high, body):
    def step(i, carry):
        body(i)
        return carry

    lax.fori_loop(low, high, step, 0)


def kernel(
    n, groups, offset, chunks,
    hidden, dkeys, weight, moment, second, gain, cosine, sine, factors,
    keys_out, weight_out, moment_out, second_out,
    h_v, dk_v, w_v, m_v, s_v, gcol, inv_v, wg_v, slices, e_all, local_v, other_v,
    part, shares, own, keys_v,
    load_sem, h_send, h_recv, e_send, e_recv, f_send, f_recv, p_send, p_recv, g_send, g_recv, out_sem,
):
    tok = h_v.shape[0]
    width = h_v.shape[1]
    feat, kvw = w_v.shape
    fc = feat // chunks
    scale = width ** (-0.5)
    me = lax.axis_index("fsdp")
    rep = lax.axis_index("rep")
    chips = n // 2
    chip = me // 2
    core = me % 2
    sibling = me + 1 - 2 * core

    loads = [
        pltpu.make_async_copy(src, dst, load_sem.at[i])
        for i, (src, dst) in enumerate(
            ((hidden, h_v), (dkeys, dk_v), (weight, w_v), (moment, m_v), (second, s_v))
        )
    ]
    for copy in loads:
        copy.start()

    barrier = pltpu.get_barrier_semaphore()

    def greet(o):
        pl.semaphore_signal(barrier, inc=1, device_id=(rep, (me + o) % n), device_id_type=MESH)

    loop(1, n, greet)
    partners = sorted({offset % groups, (groups - offset) % groups} - {0})
    for distance in partners:
        pl.semaphore_signal(
            barrier, inc=1, device_id=((rep + distance) % groups, me), device_id_type=MESH
        )
    pl.semaphore_wait(barrier, n - 1 + len(partners))

    rows_of = lambda index: pl.ds(pl.multiple_of(index * tok, tok), tok)
    chunk_of = lambda c: pl.ds(pl.multiple_of(c * fc, fc), fc)

    def own_slice(c):
        columns = pl.ds(pl.multiple_of(me * feat + c * fc, LANES), fc)
        return pltpu.make_async_copy(
            hidden.at[:, columns], slices.at[c, rows_of(me)], h_recv.at[c * n]
        )

    def slice_to(c, o):
        peer = (me + o) % n
        columns = pl.ds(pl.multiple_of(peer * feat + c * fc, LANES), fc)
        return pltpu.make_async_remote_copy(
            src_ref=hidden.at[:, columns],
            dst_ref=slices.at[c, rows_of(me)],
            send_sem=h_send.at[c * n + o],
            recv_sem=h_recv.at[c * n + o],
            device_id=(rep, peer),
            device_id_type=MESH,
        )

    def send_chunk(c):
        loop(1, n, lambda o: slice_to(c, o).start())
        own_slice(c).start()

    def wait_chunk(c):
        own_slice(c).wait()
        loop(1, n, lambda o: slice_to(c, o).wait_recv())

    send_chunk(0)

    loads[0].wait()
    block = 16

    def norm(i):
        rows = pl.ds(pl.multiple_of(i * block, block), block)
        values = h_v[rows, :].astype(f32)
        mean = jnp.sum(values * values, axis=-1, keepdims=True) * (1.0 / width)
        inv_v[rows, :] = jnp.broadcast_to(lax.rsqrt(mean + 1e-05), (block, LANES))

    loop(0, tok // block, norm)
    loads[1].wait()
    heads = [slice(i * HEAD, (i + 1) * HEAD) for i in range(kvw // HEAD)]
    for head in heads:
        x = dk_v[:, head].astype(f32)
        turned = x * cosine[...] - pltpu.roll(x, HEAD // 2, 1) * sine[...]
        e_all[rows_of(me), head] = (turned * inv_v[...]).astype(bf16)

    loads[2].wait()
    tiles = feat // LANES
    for i in range(tiles):
        row = gain[pl.ds(me * tiles + i, 1), :]
        rows = slice(i * LANES, (i + 1) * LANES)
        column = jnp.broadcast_to(row, (LANES, LANES)).T
        gcol[rows, :] = column
        for head in heads:
            wg_v[rows, head] = (w_v[rows, head].astype(f32) * column).astype(bf16)

    def e_to(q):
        peer = jnp.where(q == 0, sibling, ((chip + q) % chips) * 2 + core)
        return pltpu.make_async_remote_copy(
            src_ref=e_all.at[rows_of(me)],
            dst_ref=e_all.at[rows_of(me)],
            send_sem=e_send.at[q],
            recv_sem=e_recv.at[q],
            device_id=(rep, peer),
            device_id_type=MESH,
        )

    def forward(q):
        source = ((chip + chips - q) % chips) * 2 + core
        return pltpu.make_async_remote_copy(
            src_ref=e_all.at[rows_of(source)],
            dst_ref=e_all.at[rows_of(source)],
            send_sem=f_send.at[q],
            recv_sem=f_recv.at[q],
            device_id=(rep, sibling),
            device_id_type=MESH,
        )

    loop(1, chips, lambda q: e_to(q).start())
    e_to(0).start()
    loop(1, chunks, send_chunk)

    def relay(q):
        e_to(q).wait_recv()
        forward(q).start()

    loop(1, chips, relay)
    e_to(0).wait_recv()
    loop(1, chips, lambda q: forward(q).wait_recv())
    loads[3].wait()
    loads[4].wait()

    def gossip(c):
        rows = chunk_of(c)
        return pltpu.make_async_remote_copy(
            src_ref=local_v.at[rows],
            dst_ref=other_v.at[rows],
            send_sem=g_send.at[c],
            recv_sem=g_recv.at[c],
            device_id=((rep + offset) % groups, me),
            device_id_type=MESH,
        )

    def out_moment(c):
        return pltpu.make_async_copy(m_v.at[chunk_of(c)], moment_out.at[chunk_of(c)], out_sem.at[c])

    def out_second(c):
        return pltpu.make_async_copy(
            s_v.at[chunk_of(c)], second_out.at[chunk_of(c)], out_sem.at[chunks + c]
        )

    def out_weight(c):
        return pltpu.make_async_copy(
            (other_v if offset else local_v).at[chunk_of(c)],
            weight_out.at[chunk_of(c)],
            out_sem.at[2 * chunks + c],
        )

    def update(c):
        rows = chunk_of(c)
        total = lax.dot_general(
            slices[c], e_all[...], (((0,), (0,)), ((), ())), preferred_element_type=f32
        )
        columns = gcol[rows, :] * scale
        for head in heads:
            grad = total[:, head] * columns
            new_moment = 0.9 * m_v[rows, head] + 0.1 * grad
            new_second = 0.95 * s_v[rows, head] + 0.05 * grad * grad
            m_v[rows, head] = new_moment
            s_v[rows, head] = new_second
            w32 = w_v[rows, head].astype(f32)
            ratio = (new_moment * factors[0]) / (jnp.sqrt(new_second * factors[1]) + 1e-08)
            local_v[rows, head] = (w32 - 0.05 * (ratio + 0.1 * w32)).astype(bf16)
        out_moment(c).start()
        out_second(c).start()
        if offset:
            gossip(c).start()
        else:
            out_weight(c).start()

    def consume(c):
        wait_chunk(c)
        update(c)

    loop(0, chunks - 1, consume)
    wait_chunk(chunks - 1)

    def product(rows):
        total = jnp.zeros((tok, kvw), f32)
        for c in range(chunks):
            total += jnp.dot(
                slices[c, rows, :], wg_v[c * fc : (c + 1) * fc, :], preferred_element_type=f32
            )
        return total

    def share_to(o):
        peer = (me + o) % n
        return pltpu.make_async_remote_copy(
            src_ref=part.at[peer],
            dst_ref=shares.at[me],
            send_sem=p_send.at[o],
            recv_sem=p_recv.at[o],
            device_id=(rep, peer),
            device_id_type=MESH,
        )

    def pre_share(o):
        peer = (me + o) % n
        part[peer] = product(rows_of(peer)).astype(bf16)
        share_to(o).start()

    loop(1, n, pre_share)
    update(chunks - 1)
    own[...] = product(rows_of(me))

    def add_share(o):
        share_to(o).wait_recv()
        own[...] += shares[(me + n - o) % n].astype(f32)

    loop(1, n, add_share)
    for head in heads:
        x = own[:, head] * inv_v[...] * scale
        keys_v[:, head] = (
            x * cosine[...] + pltpu.roll(x, HEAD // 2, 1) * sine[...]
        ).astype(bf16)
    keys_copy = pltpu.make_async_copy(keys_v, keys_out, out_sem.at[3 * chunks])
    keys_copy.start()

    if offset:

        def mix(c):
            gossip(c).wait()
            rows = chunk_of(c)
            mean = (local_v[rows, :].astype(f32) + other_v[rows, :].astype(f32)) * 0.5
            other_v[rows, :] = mean.astype(bf16)
            out_weight(c).start()

        loop(0, chunks, mix)

    def drain(c):
        loop(1, n, lambda o: slice_to(c, o).wait_send())
        out_moment(c).wait()
        out_second(c).wait()
        out_weight(c).wait()

    loop(0, chunks, drain)
    loop(0, chips, lambda q: e_to(q).wait_send())
    loop(1, chips, lambda q: forward(q).wait_send())
    loop(1, n, lambda o: share_to(o).wait_send())
    keys_copy.wait()


def fused(offset, ident, n, groups, operands):
    hidden, dkeys, weight = operands[:3]
    tok, width = hidden.shape
    feat, kvw = weight.shape
    chunks = CHUNKS if feat % (CHUNKS * LANES) == 0 else max(1, feat // LANES)
    fc = feat // chunks
    chips = n // 2
    anywhere = pl.BlockSpec(memory_space=pl.ANY)
    vmem = pl.BlockSpec(memory_space=pltpu.VMEM)
    dma = pltpu.SemaphoreType.DMA
    return pl.pallas_call(
        functools.partial(kernel, n, groups, offset, chunks),
        out_shape=(
            jax.ShapeDtypeStruct((tok, kvw), bf16),
            jax.ShapeDtypeStruct((feat, kvw), bf16),
            jax.ShapeDtypeStruct((feat, kvw), f32),
            jax.ShapeDtypeStruct((feat, kvw), f32),
        ),
        in_specs=[anywhere] * 5 + [vmem] * 3 + [pl.BlockSpec(memory_space=pltpu.SMEM)],
        out_specs=(anywhere,) * 4,
        scratch_shapes=[
            pltpu.VMEM((tok, width), bf16),
            pltpu.VMEM((tok, kvw), bf16),
            pltpu.VMEM((feat, kvw), bf16),
            pltpu.VMEM((feat, kvw), f32),
            pltpu.VMEM((feat, kvw), f32),
            pltpu.VMEM((feat, LANES), f32),
            pltpu.VMEM((tok, LANES), f32),
            pltpu.VMEM((feat, kvw), bf16),
            pltpu.VMEM((chunks, n * tok, fc), bf16),
            pltpu.VMEM((n * tok, kvw), bf16),
            pltpu.VMEM((feat, kvw), bf16),
            pltpu.VMEM((feat, kvw), bf16),
            pltpu.VMEM((n, tok, kvw), bf16),
            pltpu.VMEM((n, tok, kvw), bf16),
            pltpu.VMEM((tok, kvw), f32),
            pltpu.VMEM((tok, kvw), bf16),
            dma((5,)),
            dma((chunks * n,)),
            dma((chunks * n,)),
            dma((chips,)),
            dma((chips,)),
            dma((chips,)),
            dma((chips,)),
            dma((n,)),
            dma((n,)),
            dma((chunks,)),
            dma((chunks,)),
            dma((3 * chunks + 1,)),
        ],
        compiler_params=pltpu.CompilerParams(
            collective_id=ident, has_side_effects=True, vmem_limit_bytes=60 * 2**20
        ),
    )(*operands)


def per_device(hidden, gain, key_weight, moment, second, dkeys, step):
    tok_rows, width = hidden.shape
    n = lax.axis_size("fsdp")
    groups = lax.axis_size("rep")
    positions = lax.axis_index("fsdp") * tok_rows + jnp.arange(tok_rows)
    half = HEAD // 2
    freq = jnp.exp(jnp.arange(half).astype(f32) * (-2.0 * math.log(500000.0) / HEAD))
    angle = positions.astype(f32)[:, None] * freq[None, :]
    cos, sin = jnp.cos(angle), jnp.sin(angle)
    cosine = jnp.concatenate([cos, cos], axis=-1)
    sine = jnp.concatenate([-sin, sin], axis=-1)
    count = (step + 1).astype(f32)
    factors = jnp.stack(
        [1.0 / (1.0 - jnp.power(f32(0.9), count)), 1.0 / (1.0 - jnp.power(f32(0.95), count))]
    )
    operands = (
        hidden, dkeys, key_weight[0], moment[0], second[0],
        gain.reshape(-1, LANES), cosine, sine, factors,
    )
    branches = [
        functools.partial(lambda d, i, *ops: fused(d % groups, i, n, groups, ops), d, i)
        for i, d in enumerate((1, 2, 4))
    ]
    keys, new_weight, new_moment, new_second = lax.switch(step % 3, branches, *operands)
    return (keys, new_weight[None], new_moment[None], new_second[None])


def solution(mesh):
    return jax.shard_map(
        per_device,
        mesh=mesh,
        in_specs=(
            P(("rep", "fsdp"), None),
            P(),
            P("rep", "fsdp", None),
            P("rep", "fsdp", None),
            P("rep", "fsdp", None),
            P(("rep", "fsdp"), None),
            P(),
        ),
        out_specs=(
            P(("rep", "fsdp"), None),
            P("rep", "fsdp", None),
            P("rep", "fsdp", None),
            P("rep", "fsdp", None),
        ),
        check_vma=False,
    )
```

```python
import functools
import math

import jax
import jax.numpy as jnp
from jax import lax
from jax.experimental import pallas as pl
from jax.experimental.pallas import tpu as pltpu
from jax.sharding import PartitionSpec as P

HEAD = 128
LANES = 128
CHUNKS = 4
MESH = pl.DeviceIdType.MESH
bf16 = jnp.bfloat16
f32 = jnp.float32


def loop(low, high, body):
    def step(i, carry):
        body(i)
        return carry

    lax.fori_loop(low, high, step, 0)


def kernel(
    n, groups, offset, chunks,
    hidden, dkeys, weight, moment, second, gain, cosine, sine, factors,
    keys_out, weight_out, moment_out, second_out,
    h_v, dk_v, w_v, m_v, s_v, gcol, inv_v, wg_v, slices, e_all, local_v, other_v,
    part, shares, pair_out, pair_in, mine, own, keys_v,
    load_sem, h_send, h_recv, e_send, e_recv, f_send, f_recv, s_send, s_recv, p_send, p_recv, g_send, g_recv, out_sem,
):
    tok = h_v.shape[0]
    width = h_v.shape[1]
    feat, kvw = w_v.shape
    fc = feat // chunks
    scale = width ** (-0.5)
    me = lax.axis_index("fsdp")
    rep = lax.axis_index("rep")
    chips = n // 2
    chip = me // 2
    core = me % 2
    sibling = me + 1 - 2 * core

    loads = [
        pltpu.make_async_copy(src, dst, load_sem.at[i])
        for i, (src, dst) in enumerate(
            ((hidden, h_v), (dkeys, dk_v), (weight, w_v), (moment, m_v), (second, s_v))
        )
    ]
    for copy in loads:
        copy.start()

    barrier = pltpu.get_barrier_semaphore()

    def greet(o):
        pl.semaphore_signal(barrier, inc=1, device_id=(rep, (me + o) % n), device_id_type=MESH)

    loop(1, n, greet)
    partners = sorted({offset % groups, (groups - offset) % groups} - {0})
    for distance in partners:
        pl.semaphore_signal(
            barrier, inc=1, device_id=((rep + distance) % groups, me), device_id_type=MESH
        )
    rows_of = lambda index: pl.ds(pl.multiple_of(index * tok, tok), tok)
    chunk_of = lambda c: pl.ds(pl.multiple_of(c * fc, fc), fc)

    def own_slice(c):
        columns = pl.ds(pl.multiple_of(me * feat + c * fc, LANES), fc)
        return pltpu.make_async_copy(
            hidden.at[:, columns], slices.at[c, rows_of(me)], h_recv.at[c * n + core]
        )

    def slice_to(c, q, to, by):
        peer = ((chip + q) % chips) * 2 + to
        columns = pl.ds(pl.multiple_of(peer * feat + c * fc, LANES), fc)
        return pltpu.make_async_remote_copy(
            src_ref=hidden.at[:, columns],
            dst_ref=slices.at[c, rows_of(me)],
            send_sem=h_send.at[c * n + q * 2 + to],
            recv_sem=h_recv.at[c * n + q * 2 + by],
            device_id=(rep, peer),
            device_id_type=MESH,
        )

    def send_chunk(c):
        def to_chip(q):
            slice_to(c, q, core, core).start()
            slice_to(c, q, 1 - core, core).start()

        loop(1, chips, to_chip)
        slice_to(c, 0, 1 - core, core).start()
        own_slice(c).start()

    def wait_block(c, q):
        slice_to(c, q, 0, 0).wait_recv()
        slice_to(c, q, 0, 1).wait_recv()

    def wait_own(c):
        own_slice(c).wait()
        slice_to(c, 0, 1 - core, 1 - core).wait_recv()

    def wait_chunk(c):
        wait_own(c)
        loop(1, chips, lambda q: wait_block(c, q))

    loads[0].wait()
    block = 16

    def norm(i):
        rows = pl.ds(pl.multiple_of(i * block, block), block)
        values = h_v[rows, :].astype(f32)
        mean = jnp.sum(values * values, axis=-1, keepdims=True) * (1.0 / width)
        inv_v[rows, :] = jnp.broadcast_to(lax.rsqrt(mean + 1e-05), (block, LANES))

    loop(0, tok // block, norm)
    loads[1].wait()
    heads = [slice(i * HEAD, (i + 1) * HEAD) for i in range(kvw // HEAD)]
    for head in heads:
        x = dk_v[:, head].astype(f32)
        turned = x * cosine[...] - pltpu.roll(x, HEAD // 2, 1) * sine[...]
        e_all[rows_of(me), head] = (turned * inv_v[...]).astype(bf16)

    def e_to(q):
        peer = jnp.where(q == 0, sibling, ((chip + q) % chips) * 2 + core)
        return pltpu.make_async_remote_copy(
            src_ref=e_all.at[rows_of(me)],
            dst_ref=e_all.at[rows_of(me)],
            send_sem=e_send.at[q],
            recv_sem=e_recv.at[q],
            device_id=(rep, peer),
            device_id_type=MESH,
        )

    def forward(q):
        source = ((chip + chips - q) % chips) * 2 + core
        return pltpu.make_async_remote_copy(
            src_ref=e_all.at[rows_of(source)],
            dst_ref=e_all.at[rows_of(source)],
            send_sem=f_send.at[q],
            recv_sem=f_recv.at[q],
            device_id=(rep, sibling),
            device_id_type=MESH,
        )

    pl.semaphore_wait(barrier, n - 1 + len(partners))
    loop(1, chips, lambda q: e_to(q).start())
    e_to(0).start()
    loop(0, chunks, send_chunk)

    loads[2].wait()
    tiles = feat // LANES
    for i in range(tiles):
        row = gain[pl.ds(me * tiles + i, 1), :]
        rows = slice(i * LANES, (i + 1) * LANES)
        column = jnp.broadcast_to(row, (LANES, LANES)).T
        gcol[rows, :] = column
        for head in heads:
            wg_v[rows, head] = (w_v[rows, head].astype(f32) * column).astype(bf16)

    def relay(q):
        e_to(q).wait_recv()
        forward(q).start()

    loop(1, chips, relay)
    e_to(0).wait_recv()
    loop(1, chips, lambda q: forward(q).wait_recv())
    loads[3].wait()
    loads[4].wait()

    def gossip(c):
        rows = chunk_of(c)
        return pltpu.make_async_remote_copy(
            src_ref=local_v.at[rows],
            dst_ref=other_v.at[rows],
            send_sem=g_send.at[c],
            recv_sem=g_recv.at[c],
            device_id=((rep + offset) % groups, me),
            device_id_type=MESH,
        )

    def out_moment(c):
        return pltpu.make_async_copy(m_v.at[chunk_of(c)], moment_out.at[chunk_of(c)], out_sem.at[c])

    def out_second(c):
        return pltpu.make_async_copy(
            s_v.at[chunk_of(c)], second_out.at[chunk_of(c)], out_sem.at[chunks + c]
        )

    def out_weight(c):
        return pltpu.make_async_copy(
            (other_v if offset else local_v).at[chunk_of(c)],
            weight_out.at[chunk_of(c)],
            out_sem.at[2 * chunks + c],
        )

    def update(c):
        rows = chunk_of(c)
        total = lax.dot_general(
            slices[c], e_all[...], (((0,), (0,)), ((), ())), preferred_element_type=f32
        )
        columns = gcol[rows, :] * scale
        for head in heads:
            grad = total[:, head] * columns
            new_moment = 0.9 * m_v[rows, head] + 0.1 * grad
            new_second = 0.95 * s_v[rows, head] + 0.05 * grad * grad
            m_v[rows, head] = new_moment
            s_v[rows, head] = new_second
            w32 = w_v[rows, head].astype(f32)
            ratio = (new_moment * factors[0]) / (jnp.sqrt(new_second * factors[1]) + 1e-08)
            local_v[rows, head] = (w32 - 0.05 * (ratio + 0.1 * w32)).astype(bf16)
        out_moment(c).start()
        out_second(c).start()
        if offset:
            gossip(c).start()
        else:
            out_weight(c).start()

    def consume(c):
        wait_chunk(c)
        update(c)

    loop(0, chunks - 1, consume)

    def product(rows):
        total = jnp.zeros((tok, kvw), f32)
        for c in range(chunks):
            total += jnp.dot(
                slices[c, rows, :], wg_v[c * fc : (c + 1) * fc, :], preferred_element_type=f32
            )
        return total

    def to_sibling(q):
        return pltpu.make_async_remote_copy(
            src_ref=pair_out.at[q],
            dst_ref=pair_in.at[q],
            send_sem=s_send.at[q],
            recv_sem=s_recv.at[q],
            device_id=(rep, sibling),
            device_id_type=MESH,
        )

    def share_to(q):
        return pltpu.make_async_remote_copy(
            src_ref=part.at[q],
            dst_ref=shares.at[q],
            send_sem=p_send.at[q],
            recv_sem=p_recv.at[q],
            device_id=(rep, ((chip + chips - q) % chips) * 2 + core),
            device_id_type=MESH,
        )

    def products(q):
        source = ((chip + chips - q) % chips) * 2
        pair_out[q] = product(rows_of(source + 1 - core))
        to_sibling(q).start()
        mine[q] = product(rows_of(source + core))

    def pre_share(q):
        to_sibling(q).wait_recv()
        part[q] = (mine[q] + pair_in[q]).astype(bf16)
        share_to(q).start()

    def arrived(q):
        wait_block(chunks - 1, q)
        products(q)

    wait_own(chunks - 1)
    products(0)
    arrived(1)

    def steady(q):
        arrived(q)
        pre_share(q - 1)

    loop(2, chips, steady)
    pre_share(chips - 1)
    update(chunks - 1)
    to_sibling(0).wait_recv()
    own[...] = mine[0] + pair_in[0]

    def add_share(q):
        share_to(q).wait_recv()
        own[...] += shares[q].astype(f32)

    loop(1, chips, add_share)
    for head in heads:
        x = own[:, head] * inv_v[...] * scale
        keys_v[:, head] = (
            x * cosine[...] + pltpu.roll(x, HEAD // 2, 1) * sine[...]
        ).astype(bf16)
    keys_copy = pltpu.make_async_copy(keys_v, keys_out, out_sem.at[3 * chunks])
    keys_copy.start()

    if offset:

        def mix(c):
            gossip(c).wait()
            rows = chunk_of(c)
            mean = (local_v[rows, :].astype(f32) + other_v[rows, :].astype(f32)) * 0.5
            other_v[rows, :] = mean.astype(bf16)
            out_weight(c).start()

        loop(0, chunks, mix)

    def drain(c):
        slice_to(c, 0, 1 - core, core).wait_send()
        loop(2, n, lambda i: slice_to(c, i // 2, i % 2, core).wait_send())
        out_moment(c).wait()
        out_second(c).wait()
        out_weight(c).wait()

    loop(0, chunks, drain)
    loop(0, chips, lambda q: e_to(q).wait_send())
    loop(1, chips, lambda q: forward(q).wait_send())
    loop(1, chips, lambda q: share_to(q).wait_send())
    loop(0, chips, lambda q: to_sibling(q).wait_send())
    keys_copy.wait()


def fused(offset, ident, n, groups, operands):
    hidden, dkeys, weight = operands[:3]
    tok, width = hidden.shape
    feat, kvw = weight.shape
    chunks = CHUNKS if feat % (CHUNKS * LANES) == 0 else max(1, feat // LANES)
    fc = feat // chunks
    chips = n // 2
    anywhere = pl.BlockSpec(memory_space=pl.ANY)
    vmem = pl.BlockSpec(memory_space=pltpu.VMEM)
    dma = pltpu.SemaphoreType.DMA
    return pl.pallas_call(
        functools.partial(kernel, n, groups, offset, chunks),
        out_shape=(
            jax.ShapeDtypeStruct((tok, kvw), bf16),
            jax.ShapeDtypeStruct((feat, kvw), bf16),
            jax.ShapeDtypeStruct((feat, kvw), f32),
            jax.ShapeDtypeStruct((feat, kvw), f32),
        ),
        in_specs=[pl.BlockSpec(memory_space=pltpu.HBM)] * 5 + [vmem] * 3 + [pl.BlockSpec(memory_space=pltpu.SMEM)],
        out_specs=(anywhere,) * 4,
        scratch_shapes=[
            pltpu.VMEM((tok, width), bf16),
            pltpu.VMEM((tok, kvw), bf16),
            pltpu.VMEM((feat, kvw), bf16),
            pltpu.VMEM((feat, kvw), f32),
            pltpu.VMEM((feat, kvw), f32),
            pltpu.VMEM((feat, LANES), f32),
            pltpu.VMEM((tok, LANES), f32),
            pltpu.VMEM((feat, kvw), bf16),
            pltpu.VMEM((chunks, n * tok, fc), bf16),
            pltpu.VMEM((n * tok, kvw), bf16),
            pltpu.VMEM((feat, kvw), bf16),
            pltpu.VMEM((feat, kvw), bf16),
            pltpu.VMEM((chips, tok, kvw), bf16),
            pltpu.VMEM((chips, tok, kvw), bf16),
            pltpu.VMEM((chips, tok, kvw), f32),
            pltpu.VMEM((chips, tok, kvw), f32),
            pltpu.VMEM((chips, tok, kvw), f32),
            pltpu.VMEM((tok, kvw), f32),
            pltpu.VMEM((tok, kvw), bf16),
            dma((5,)),
            dma((chunks * n,)),
            dma((chunks * n,)),
            dma((chips,)),
            dma((chips,)),
            dma((chips,)),
            dma((chips,)),
            dma((chips,)),
            dma((chips,)),
            dma((chips,)),
            dma((chips,)),
            dma((chunks,)),
            dma((chunks,)),
            dma((3 * chunks + 1,)),
        ],
        compiler_params=pltpu.CompilerParams(
            collective_id=ident, has_side_effects=True, vmem_limit_bytes=38 * 2**20
        ),
    )(*operands)


def per_device(hidden, gain, key_weight, moment, second, dkeys, step):
    tok_rows, width = hidden.shape
    n = lax.axis_size("fsdp")
    groups = lax.axis_size("rep")
    positions = lax.axis_index("fsdp") * tok_rows + jnp.arange(tok_rows)
    half = HEAD // 2
    freq = jnp.exp(jnp.arange(half).astype(f32) * (-2.0 * math.log(500000.0) / HEAD))
    angle = positions.astype(f32)[:, None] * freq[None, :]
    cos, sin = jnp.cos(angle), jnp.sin(angle)
    cosine = jnp.concatenate([cos, cos], axis=-1)
    sine = jnp.concatenate([-sin, sin], axis=-1)
    count = (step + 1).astype(f32)
    factors = jnp.stack(
        [1.0 / (1.0 - jnp.power(f32(0.9), count)), 1.0 / (1.0 - jnp.power(f32(0.95), count))]
    )
    operands = (
        hidden, dkeys, key_weight[0], moment[0], second[0],
        gain.reshape(-1, LANES), cosine, sine, factors,
    )
    branches = [
        functools.partial(lambda d, i, *ops: fused(d % groups, i, n, groups, ops), d, i)
        for i, d in enumerate((1, 2, 4))
    ]
    keys, new_weight, new_moment, new_second = lax.switch(step % 3, branches, *operands)
    return (keys, new_weight[None], new_moment[None], new_second[None])


def solution(mesh):
    return jax.shard_map(
        per_device,
        mesh=mesh,
        in_specs=(
            P(("rep", "fsdp"), None),
            P(),
            P("rep", "fsdp", None),
            P("rep", "fsdp", None),
            P("rep", "fsdp", None),
            P(("rep", "fsdp"), None),
            P(),
        ),
        out_specs=(
            P(("rep", "fsdp"), None),
            P("rep", "fsdp", None),
            P("rep", "fsdp", None),
            P("rep", "fsdp", None),
        ),
        check_vma=False,
    )
```

```python
import functools
import math

import jax
import jax.numpy as jnp
from jax import lax
from jax.experimental import pallas as pl
from jax.experimental.pallas import tpu as pltpu
from jax.sharding import PartitionSpec as P

HEAD = 128
LANES = 128
MESH = pl.DeviceIdType.MESH
bf16 = jnp.bfloat16
f32 = jnp.float32


def loop(low, high, body):
    def step(i, carry):
        body(i)
        return carry

    lax.fori_loop(low, high, step, 0)


def kernel(
    n, groups, offset, starts,
    hidden, dkeys, weight, moment, second, gain, cosine, sine, factors,
    keys_out, weight_out, moment_out, second_out,
    h_v, dk_v, w_v, m_v, s_v, gcol, inv_v, wg_v, slices, e_all, local_v, other_v,
    part, shares, pair_out, pair_in, mine, own, keys_v,
    load_sem, h_send, h_recv, e_send, e_recv, f_send, f_recv, s_send, s_recv, p_send, p_recv, g_send, g_recv, out_sem,
):
    tok = h_v.shape[0]
    chunks = len(starts) - 1
    width = h_v.shape[1]
    feat, kvw = w_v.shape
    scale = width ** (-0.5)
    me = lax.axis_index("fsdp")
    rep = lax.axis_index("rep")
    chips = n // 2
    chip = me // 2
    core = me % 2
    sibling = me + 1 - 2 * core

    loads = [
        pltpu.make_async_copy(src, dst, load_sem.at[i])
        for i, (src, dst) in enumerate(
            ((hidden, h_v), (dkeys, dk_v), (weight, w_v), (moment, m_v), (second, s_v))
        )
    ]
    for copy in loads:
        copy.start()

    barrier = pltpu.get_barrier_semaphore()

    def greet(o):
        pl.semaphore_signal(barrier, inc=1, device_id=(rep, (me + o) % n), device_id_type=MESH)

    loop(1, n, greet)
    partners = sorted({offset % groups, (groups - offset) % groups} - {0})
    for distance in partners:
        pl.semaphore_signal(
            barrier, inc=1, device_id=((rep + distance) % groups, me), device_id_type=MESH
        )
    rows_of = lambda index: pl.ds(pl.multiple_of(index * tok, tok), tok)
    chunk_of = lambda c: slice(starts[c], starts[c + 1])

    def own_slice(c):
        columns = pl.ds(pl.multiple_of(me * feat + starts[c], LANES), starts[c + 1] - starts[c])
        return pltpu.make_async_copy(
            hidden.at[:, columns], slices.at[rows_of(me), chunk_of(c)], h_recv.at[c * n + core]
        )

    def slice_to(c, q, to, by):
        peer = ((chip + q) % chips) * 2 + to
        columns = pl.ds(pl.multiple_of(peer * feat + starts[c], LANES), starts[c + 1] - starts[c])
        return pltpu.make_async_remote_copy(
            src_ref=hidden.at[:, columns],
            dst_ref=slices.at[rows_of(me), chunk_of(c)],
            send_sem=h_send.at[c * n + q * 2 + to],
            recv_sem=h_recv.at[c * n + q * 2 + by],
            device_id=(rep, peer),
            device_id_type=MESH,
        )

    def send_chunk(c):
        def to_chip(q):
            slice_to(c, q, core, core).start()
            slice_to(c, q, 1 - core, core).start()

        loop(1, chips, to_chip)
        slice_to(c, 0, 1 - core, core).start()
        own_slice(c).start()

    def wait_block(c, q):
        slice_to(c, q, 0, 0).wait_recv()
        slice_to(c, q, 0, 1).wait_recv()

    def wait_own(c):
        own_slice(c).wait()
        slice_to(c, 0, 1 - core, 1 - core).wait_recv()

    def wait_chunk(c):
        wait_own(c)
        loop(1, chips, lambda q: wait_block(c, q))

    pl.semaphore_wait(barrier, n - 1 + len(partners))
    send_chunk(0)

    loads[0].wait()
    block = 16

    def norm(i):
        rows = pl.ds(pl.multiple_of(i * block, block), block)
        values = h_v[rows, :].astype(f32)
        mean = jnp.sum(values * values, axis=-1, keepdims=True) * (1.0 / width)
        inv_v[rows, :] = jnp.broadcast_to(lax.rsqrt(mean + 1e-05), (block, LANES))

    loop(0, tok // block, norm)
    loads[1].wait()
    heads = [slice(i * HEAD, (i + 1) * HEAD) for i in range(kvw // HEAD)]
    for head in heads:
        x = dk_v[:, head].astype(f32)
        turned = x * cosine[...] - pltpu.roll(x, HEAD // 2, 1) * sine[...]
        e_all[rows_of(me), head] = (turned * inv_v[...]).astype(bf16)

    def e_to(q):
        peer = jnp.where(q == 0, sibling, ((chip + q) % chips) * 2 + core)
        return pltpu.make_async_remote_copy(
            src_ref=e_all.at[rows_of(me)],
            dst_ref=e_all.at[rows_of(me)],
            send_sem=e_send.at[q],
            recv_sem=e_recv.at[q],
            device_id=(rep, peer),
            device_id_type=MESH,
        )

    def forward(q):
        source = ((chip + chips - q) % chips) * 2 + core
        return pltpu.make_async_remote_copy(
            src_ref=e_all.at[rows_of(source)],
            dst_ref=e_all.at[rows_of(source)],
            send_sem=f_send.at[q],
            recv_sem=f_recv.at[q],
            device_id=(rep, sibling),
            device_id_type=MESH,
        )

    loop(1, chips, lambda q: e_to(q).start())
    e_to(0).start()
    for c in range(1, chunks):
        send_chunk(c)

    loads[2].wait()
    tiles = feat // LANES
    for i in range(tiles):
        row = gain[pl.ds(me * tiles + i, 1), :]
        rows = slice(i * LANES, (i + 1) * LANES)
        column = jnp.broadcast_to(row, (LANES, LANES)).T
        gcol[rows, :] = column
        for head in heads:
            wg_v[rows, head] = (w_v[rows, head].astype(f32) * column).astype(bf16)

    def relay(q):
        e_to(q).wait_recv()
        forward(q).start()

    loop(1, chips, relay)
    e_to(0).wait_recv()
    loop(1, chips, lambda q: forward(q).wait_recv())
    loads[3].wait()
    loads[4].wait()

    def gossip(c):
        rows = chunk_of(c)
        return pltpu.make_async_remote_copy(
            src_ref=local_v.at[rows],
            dst_ref=other_v.at[rows],
            send_sem=g_send.at[c],
            recv_sem=g_recv.at[c],
            device_id=((rep + offset) % groups, me),
            device_id_type=MESH,
        )

    def out_moment(c):
        return pltpu.make_async_copy(m_v.at[chunk_of(c)], moment_out.at[chunk_of(c)], out_sem.at[c])

    def out_second(c):
        return pltpu.make_async_copy(
            s_v.at[chunk_of(c)], second_out.at[chunk_of(c)], out_sem.at[chunks + c]
        )

    def out_weight(c):
        return pltpu.make_async_copy(
            (other_v if offset else local_v).at[chunk_of(c)],
            weight_out.at[chunk_of(c)],
            out_sem.at[2 * chunks + c],
        )

    def update(c):
        rows = chunk_of(c)
        total = lax.dot_general(
            slices[:, rows], e_all[...], (((0,), (0,)), ((), ())), preferred_element_type=f32
        )
        columns = gcol[rows, :] * scale
        for head in heads:
            grad = total[:, head] * columns
            new_moment = 0.9 * m_v[rows, head] + 0.1 * grad
            new_second = 0.95 * s_v[rows, head] + 0.05 * grad * grad
            m_v[rows, head] = new_moment
            s_v[rows, head] = new_second
            w32 = w_v[rows, head].astype(f32)
            ratio = (new_moment * factors[0]) / (jnp.sqrt(new_second * factors[1]) + 1e-08)
            local_v[rows, head] = (w32 - 0.05 * (ratio + 0.1 * w32)).astype(bf16)
        out_moment(c).start()
        out_second(c).start()
        if offset:
            gossip(c).start()
        else:
            out_weight(c).start()

    def consume(c):
        wait_chunk(c)
        update(c)

    for c in range(chunks - 1):
        consume(c)

    def product(rows):
        return jnp.dot(slices[rows, :], wg_v[...], preferred_element_type=f32)

    def to_sibling(q):
        return pltpu.make_async_remote_copy(
            src_ref=pair_out.at[q],
            dst_ref=pair_in.at[q],
            send_sem=s_send.at[q],
            recv_sem=s_recv.at[q],
            device_id=(rep, sibling),
            device_id_type=MESH,
        )

    def share_to(q):
        return pltpu.make_async_remote_copy(
            src_ref=part.at[q],
            dst_ref=shares.at[q],
            send_sem=p_send.at[q],
            recv_sem=p_recv.at[q],
            device_id=(rep, ((chip + chips - q) % chips) * 2 + core),
            device_id_type=MESH,
        )

    def products(q):
        source = ((chip + chips - q) % chips) * 2
        pair_out[q] = product(rows_of(source + 1 - core))
        to_sibling(q).start()
        mine[q] = product(rows_of(source + core))

    def pre_share(q):
        to_sibling(q).wait_recv()
        part[q] = (mine[q] + pair_in[q]).astype(bf16)
        share_to(q).start()

    def arrived(q):
        wait_block(chunks - 1, q)
        products(q)

    wait_own(chunks - 1)
    products(0)
    arrived(1)

    def steady(q):
        arrived(q)
        pre_share(q - 1)

    loop(2, chips, steady)
    pre_share(chips - 1)
    update(chunks - 1)
    to_sibling(0).wait_recv()
    own[...] = mine[0] + pair_in[0]

    def add_share(q):
        share_to(q).wait_recv()
        own[...] += shares[q].astype(f32)

    loop(1, chips, add_share)
    for head in heads:
        x = own[:, head] * inv_v[...] * scale
        keys_v[:, head] = (
            x * cosine[...] + pltpu.roll(x, HEAD // 2, 1) * sine[...]
        ).astype(bf16)
    keys_copy = pltpu.make_async_copy(keys_v, keys_out, out_sem.at[3 * chunks])
    keys_copy.start()

    if offset:

        def mix(c):
            gossip(c).wait()
            rows = chunk_of(c)
            mean = (local_v[rows, :].astype(f32) + other_v[rows, :].astype(f32)) * 0.5
            other_v[rows, :] = mean.astype(bf16)
            out_weight(c).start()

        for c in range(chunks):
            mix(c)

    def drain(c):
        slice_to(c, 0, 1 - core, core).wait_send()
        loop(2, n, lambda i: slice_to(c, i // 2, i % 2, core).wait_send())
        out_moment(c).wait()
        out_second(c).wait()
        out_weight(c).wait()

    for c in range(chunks):
        drain(c)
    loop(0, chips, lambda q: e_to(q).wait_send())
    loop(1, chips, lambda q: forward(q).wait_send())
    loop(1, chips, lambda q: share_to(q).wait_send())
    loop(0, chips, lambda q: to_sibling(q).wait_send())
    keys_copy.wait()


def bounds(feat):
    return (0, *range(LANES, feat - LANES, 2 * LANES), feat - LANES, feat)


def flush_kernel(*refs):
    half = len(refs[:-1]) // 2
    copies = []
    for src, dst in zip(refs[:half], refs[half:-1]):
        pieces = max(1, src.size * src.dtype.itemsize // 2**19)
        rows = src.shape[0] // pieces
        for i in range(pieces):
            part = pl.ds(i * rows, rows)
            copies.append((src.at[part], dst.at[part]))
    copies = [
        pltpu.make_async_copy(src, dst, refs[-1].at[i]) for i, (src, dst) in enumerate(copies)
    ]
    for copy in copies:
        copy.start()
    for copy in copies:
        copy.wait()


def flush(arrays):
    count = sum(max(1, a.size * a.dtype.itemsize // 2**19) for a in arrays)
    return pl.pallas_call(
        flush_kernel,
        out_shape=tuple(jax.ShapeDtypeStruct(a.shape, a.dtype) for a in arrays),
        in_specs=[pl.BlockSpec(memory_space=pl.ANY)] * len(arrays),
        out_specs=(pl.BlockSpec(memory_space=pltpu.HBM),) * len(arrays),
        scratch_shapes=[pltpu.SemaphoreType.DMA((count,))],
        compiler_params=pltpu.CompilerParams(vmem_limit_bytes=2**20),
    )(*arrays)


def fused(offset, ident, n, groups, operands):
    hidden, dkeys, weight = operands[:3]
    tok, width = hidden.shape
    feat, kvw = weight.shape
    starts = bounds(feat)
    chunks = len(starts) - 1
    chips = n // 2
    anywhere = pl.BlockSpec(memory_space=pl.ANY)
    vmem = pl.BlockSpec(memory_space=pltpu.VMEM)
    dma = pltpu.SemaphoreType.DMA
    return pl.pallas_call(
        functools.partial(kernel, n, groups, offset, starts),
        out_shape=(
            jax.ShapeDtypeStruct((tok, kvw), bf16),
            jax.ShapeDtypeStruct((feat, kvw), bf16),
            jax.ShapeDtypeStruct((feat, kvw), f32),
            jax.ShapeDtypeStruct((feat, kvw), f32),
        ),
        in_specs=[pl.BlockSpec(memory_space=pltpu.HBM)] * 5 + [vmem] * 3 + [pl.BlockSpec(memory_space=pltpu.SMEM)],
        out_specs=(anywhere,) * 4,
        scratch_shapes=[
            pltpu.VMEM((tok, width), bf16),
            pltpu.VMEM((tok, kvw), bf16),
            pltpu.VMEM((feat, kvw), bf16),
            pltpu.VMEM((feat, kvw), f32),
            pltpu.VMEM((feat, kvw), f32),
            pltpu.VMEM((feat, LANES), f32),
            pltpu.VMEM((tok, LANES), f32),
            pltpu.VMEM((feat, kvw), bf16),
            pltpu.VMEM((n * tok, feat), bf16),
            pltpu.VMEM((n * tok, kvw), bf16),
            pltpu.VMEM((feat, kvw), bf16),
            pltpu.VMEM((feat, kvw), bf16),
            pltpu.VMEM((chips, tok, kvw), bf16),
            pltpu.VMEM((chips, tok, kvw), bf16),
            pltpu.VMEM((chips, tok, kvw), f32),
            pltpu.VMEM((chips, tok, kvw), f32),
            pltpu.VMEM((chips, tok, kvw), f32),
            pltpu.VMEM((tok, kvw), f32),
            pltpu.VMEM((tok, kvw), bf16),
            dma((5,)),
            dma((chunks * n,)),
            dma((chunks * n,)),
            dma((chips,)),
            dma((chips,)),
            dma((chips,)),
            dma((chips,)),
            dma((chips,)),
            dma((chips,)),
            dma((chips,)),
            dma((chips,)),
            dma((chunks,)),
            dma((chunks,)),
            dma((3 * chunks + 1,)),
        ],
        compiler_params=pltpu.CompilerParams(
            collective_id=ident, has_side_effects=True, vmem_limit_bytes=38 * 2**20
        ),
    )(*operands)


def per_device(hidden, gain, key_weight, moment, second, dkeys, step):
    tok_rows, width = hidden.shape
    n = lax.axis_size("fsdp")
    groups = lax.axis_size("rep")
    positions = lax.axis_index("fsdp") * tok_rows + jnp.arange(tok_rows)
    half = HEAD // 2
    freq = jnp.exp(jnp.arange(half).astype(f32) * (-2.0 * math.log(500000.0) / HEAD))
    angle = positions.astype(f32)[:, None] * freq[None, :]
    cos, sin = jnp.cos(angle), jnp.sin(angle)
    cosine = jnp.concatenate([cos, cos], axis=-1)
    sine = jnp.concatenate([-sin, sin], axis=-1)
    count = (step + 1).astype(f32)
    factors = jnp.stack(
        [1.0 / (1.0 - jnp.power(f32(0.9), count)), 1.0 / (1.0 - jnp.power(f32(0.95), count))]
    )
    operands = (
        hidden, dkeys, key_weight[0], moment[0], second[0],
        gain.reshape(-1, LANES), cosine, sine, factors,
    )
    branches = [
        functools.partial(lambda d, i, *ops: fused(d % groups, i, n, groups, ops), d, i)
        for i, d in enumerate((1, 2, 4))
    ]
    keys, new_weight, new_moment, new_second = lax.switch(step % 3, branches, *operands)
    keys, new_weight, new_moment = flush((keys, new_weight, new_moment))
    return (keys, new_weight[None], new_moment[None], new_second[None])


def solution(mesh):
    return jax.shard_map(
        per_device,
        mesh=mesh,
        in_specs=(
            P(("rep", "fsdp"), None),
            P(),
            P("rep", "fsdp", None),
            P("rep", "fsdp", None),
            P("rep", "fsdp", None),
            P(("rep", "fsdp"), None),
            P(),
        ),
        out_specs=(
            P(("rep", "fsdp"), None),
            P("rep", "fsdp", None),
            P("rep", "fsdp", None),
            P("rep", "fsdp", None),
        ),
        check_vma=False,
    )
```
